32 devices in a mesh: groups: 2 (over y), seq: 16 (over z, x, core).
Axes of the slice: x: 2, y: 2, z: 4, core: 2. Of those that a mesh axis runs over, the one named last changes fastest.
Arguments:
- xbc: bfloat16 [16384, 2304], P(('groups', 'seq')), parts along dimension 0, may hold values from -24 to 24
- conv_weight: float32 [4, 2304], replicated, may hold values from -3 to 3
- log_decay: float32 [16, 16384], P(None, ('groups', 'seq')), parts along dimension 1, may hold values from -1 to 0, as said below
- level_weights: float32 [16, 14, 16384], P(None, None, ('groups', 'seq')), parts along dimension 2, may hold values from 0.1 to 1
- gain: float32 [2048], replicated, may hold values from 0.25 to 1.75
Outputs:
- mixed: bfloat16 [16384, 2048], P(('groups', 'seq')), parts along dimension 0
The draws below stay inside these ranges and needn't reach their ends.
There are 2 independent parts, one for each index of `groups`. The reference program is written for one: setup_inputs(seed, part) draws one part's arguments, and reference() takes and returns one part's arrays. A program takes and returns all parts, laid end to end along the dimension named above; an argument that names none is the same for every part. Nothing has to cross between parts.
Inputs may be any that keep to these rules, and one draw needn't show every extreme that they name: `log_decay`: every entry is negative.
All inputs are finite; a program needn't handle non-finite values.
Results may differ from the reference program's by a relative error of at most 0.0034.
Values may be sent and summed in bfloat16 or wider, within the bound.
A program may use at most 128 MiB of HBM per device.

```python
import math
import jax
import jax.numpy as jnp
from jax import lax

PAIRED_MIXER_NUM = 16
HEAD_DIM = 128
STATE = 128
KERNEL = 4
TOK_DEV = 512
INNER = 2048
WIDTH = 2304
STEP_AMOUNT = 8192
LOG_TOK = 9
LOG_SEQ = 4
LEVELS = 14


def draw_xbc(key, part):
    key_base, key_cols, key_rows = jax.random.split(key, 3)
    col_scale = jnp.exp(jax.random.uniform(key_cols, (1, WIDTH), jnp.float32, math.log(0.4), math.log(4.0)))
    row_scale = jnp.exp(jax.random.uniform(key_rows, (STEP_AMOUNT, 1), jnp.float32, math.log(0.5), math.log(2.0)))
    entries = jax.random.normal(key_base, (STEP_AMOUNT, WIDTH), jnp.float32) * col_scale * row_scale
    return jnp.clip(entries, -24.0, 24.0).astype(jnp.bfloat16)


def draw_log_decay(key, part):
    lookup_vectors = jax.random.split(key, 9)
    head_kind = jax.random.randint(lookup_vectors[0], (PAIRED_MIXER_NUM, 1), 0, 4)
    fast_rate = jnp.exp(jax.random.uniform(lookup_vectors[2], (PAIRED_MIXER_NUM, 1), jnp.float32, math.log(1.0 / 50.0), math.log(1.0 / 30.0)))
    medium_rate = jnp.exp(jax.random.uniform(lookup_vectors[3], (PAIRED_MIXER_NUM, 1), jnp.float32, math.log(0.5), math.log(2.0))) / TOK_DEV
    slow_rate = jnp.exp(jax.random.uniform(lookup_vectors[4], (PAIRED_MIXER_NUM, 1), jnp.float32, math.log(0.1), math.log(0.4))) / STEP_AMOUNT
    channel_forget_factor = jnp.where(head_kind == 0, fast_rate, jnp.where(head_kind == 1, medium_rate, slow_rate))
    segment_factor = jnp.exp(jax.random.uniform(lookup_vectors[5], (PAIRED_MIXER_NUM, STEP_AMOUNT // TOK_DEV), jnp.float32, math.log(0.5), math.log(2.0)))
    segment_factor = jnp.repeat(segment_factor, TOK_DEV, axis=1)
    element_factor = jnp.exp(jax.random.uniform(lookup_vectors[6], (PAIRED_MIXER_NUM, STEP_AMOUNT), jnp.float32, math.log(0.5), math.log(2.0)))
    segment_offset = jax.random.randint(lookup_vectors[7], (PAIRED_MIXER_NUM, 3, 1), 0, STEP_AMOUNT)
    segment_size = jax.random.uniform(lookup_vectors[8], (PAIRED_MIXER_NUM, 3, 1), jnp.float32, 0.22, 0.5)
    element_index = lax.iota(jnp.int32, STEP_AMOUNT)[None, None, :]
    segment_list = jnp.sum(jnp.where(element_index == segment_offset, segment_size, 0.0), axis=1)
    return -(channel_forget_factor * segment_factor * element_factor + segment_list)


def steps_of(key, shape, cuts, least, largest):
    loudness, own = 1.0, jax.random.fold_in(key, 6)
    for dim, parts in cuts:
        heights = jnp.exp(jax.random.uniform(jax.random.fold_in(own, dim), (parts,), jnp.float32, least / len(cuts), largest / len(cuts)))
        loudness = loudness * jnp.repeat(heights, shape[dim] // parts).reshape([-1 if axis == dim else 1 for axis in range(len(shape))])
    return loudness


def gaussian(rng, extent, spread, most, held_as=jnp.bfloat16):
    drawn = jax.random.normal(rng, extent, jnp.float32) * spread
    return jnp.minimum(jnp.maximum(drawn, -most), most).astype(held_as)


def setup_inputs(seed: int = 0, part: int = 0) -> dict:
    keys = jax.random.split(jax.random.key(seed), 6)
    own_keys = jax.random.split(jax.random.fold_in(keys[5], part), 6)
    return {
        "xbc": draw_xbc(jax.random.fold_in(jax.random.fold_in(keys[5], part), 71), part),
        "conv_weight": gaussian(keys[1], (KERNEL, WIDTH), KERNEL ** -0.5, 3.0, jnp.float32),
        "log_decay": draw_log_decay(jax.random.fold_in(jax.random.fold_in(keys[5], part), 71), part),
        "level_weights": jnp.clip(jnp.exp(math.log(1.0) - 2.3025851 * jax.random.uniform(own_keys[3], (PAIRED_MIXER_NUM, LEVELS, STEP_AMOUNT), jnp.float32) ** steps_of(own_keys[3], (PAIRED_MIXER_NUM, LEVELS, STEP_AMOUNT), ((2, 16),), -0.2, 0.2)), 0.1, 1.0),
        "gain": jnp.clip(1.0 + 0.15 * jax.random.normal(keys[4], (INNER,), jnp.float32), 0.25, 1.75),
    }


def bit_length(numbers, limit):
    counted = jnp.zeros(numbers.shape, jnp.int32)
    for power_index in range(limit):
        counted = counted + (numbers >= 1 << power_index).astype(jnp.int32)
    return counted

def compute_near(values_rows, in_map, out_map, local_log, level_gain, head_count):
    row_count = values_rows.shape[0]
    head_dim = values_rows.shape[1] // head_count
    local_bits = row_count.bit_length() - 1
    scores = jnp.dot(out_map, in_map.T, preferred_element_type=jnp.float32)
    element_index = lax.iota(jnp.int32, row_count)
    level_index = bit_length(jnp.bitwise_xor(element_index[:, None], element_index[None, :]), local_bits)
    causal = element_index[None, :] <= element_index[:, None]
    chosen = jnp.zeros((head_count, row_count, row_count), jnp.float32)
    for level_step in range(local_bits + 1):
        chosen = jnp.where((level_index == level_step)[None], level_gain[:, level_step, :, None], chosen)
    gap_log = jnp.where(causal[None], local_log[:, :, None] - local_log[:, None, :], -1e+30)
    weight = (chosen * jnp.exp(gap_log) * scores[None]).astype(jnp.bfloat16)
    shaped = values_rows.reshape(row_count, head_count, head_dim).astype(jnp.float32)
    near_heads = jnp.einsum('hts,shp->thp', weight.astype(jnp.float32), shaped)
    return near_heads.reshape(row_count, head_count * head_dim)

def reference(xbc, conv_weight, log_decay, level_weights, gain):
    inner_width = PAIRED_MIXER_NUM * HEAD_DIM
    blocks = STEP_AMOUNT // TOK_DEV
    padded = jnp.concatenate([jnp.zeros((KERNEL - 1, xbc.shape[1]), jnp.float32), xbc.astype(jnp.float32)], axis=0)
    convolved = padded[0:STEP_AMOUNT] * conv_weight[0]
    for offset in range(1, KERNEL):
        convolved = convolved + padded[offset:offset + STEP_AMOUNT] * conv_weight[offset]
    activated = jax.nn.silu(convolved).astype(jnp.bfloat16)
    values_all = activated[:, :inner_width].reshape(blocks, TOK_DEV, inner_width)
    in_all = activated[:, inner_width:inner_width + STATE].reshape(blocks, TOK_DEV, STATE)
    out_all = activated[:, inner_width + STATE:].reshape(blocks, TOK_DEV, STATE)
    local_log = jnp.cumsum(log_decay.reshape(PAIRED_MIXER_NUM, blocks, TOK_DEV), axis=2)
    block_total = local_log[:, :, TOK_DEV - 1]
    inclusive = jnp.cumsum(block_total, axis=1)
    before = inclusive - block_total

    def state_of(pieces):
        values_block, in_block, log_block, total_block = pieces
        tail_decay = jnp.exp(total_block[:, None] - log_block)
        decayed = (values_block.reshape(TOK_DEV, PAIRED_MIXER_NUM, HEAD_DIM) * tail_decay.T[:, :, None]).reshape(TOK_DEV, inner_width).astype(jnp.bfloat16)
        return jnp.dot(in_block.T, decayed, preferred_element_type=jnp.float32)
    states = lax.map(state_of, (values_all, in_all, local_log.transpose(1, 0, 2), block_total.T))
    group_list = []
    for level_index in range(1, LOG_SEQ + 1):
        group_span = 2 ** (level_index - 1)
        group_count = blocks // group_span
        grouped = states.reshape(group_count, group_span, STATE, PAIRED_MIXER_NUM, HEAD_DIM)
        ends_log = inclusive.reshape(PAIRED_MIXER_NUM, group_count, group_span)
        weight = jnp.exp(ends_log[:, :, group_span - 1:group_span] - ends_log)
        level_node = jnp.einsum('hgm,gmnhp->gnhp', weight, grouped, precision=lax.Precision.HIGHEST)
        group_list.append((level_node.reshape(group_count, STATE, inner_width), ends_log[:, :, group_span - 1]))

    def output_of(pieces):
        block_index, values_block, in_block, out_block, log_block, gain_block, start_log = pieces
        near_term = compute_near(values_block, in_block, out_block, log_block, gain_block, PAIRED_MIXER_NUM)
        far_term = jnp.zeros((TOK_DEV, inner_width), jnp.float32)
        queries_wide = out_block.astype(jnp.float32)
        for level_index in range(1, LOG_SEQ + 1):
            node_all, group_ends = group_list[level_index - 1]
            is_upper = block_index >> level_index - 1 & 1 == 1
            group_slot = jnp.maximum((block_index >> level_index - 1) - 1, 0).astype(jnp.int32)
            level_node = node_all[group_slot]
            gap_log = start_log - group_ends[:, group_slot]
            exponent = jnp.where(is_upper, log_block + gap_log[:, None], -1e+30)
            factor = gain_block[:, LOG_TOK + level_index, :] * jnp.exp(exponent)
            product = jnp.dot(queries_wide, level_node, precision=lax.Precision.HIGHEST)
            far_term = far_term + (product.reshape(TOK_DEV, PAIRED_MIXER_NUM, HEAD_DIM) * factor.T[:, :, None]).reshape(TOK_DEV, inner_width)
        mixed_sum = (near_term + far_term).reshape(TOK_DEV, PAIRED_MIXER_NUM, HEAD_DIM)
        inv_rms = lax.rsqrt(lax.optimization_barrier(jnp.mean(mixed_sum * mixed_sum, axis=2, keepdims=True)) + 1e-05)
        return ((mixed_sum * inv_rms).reshape(TOK_DEV, inner_width) * gain).astype(jnp.bfloat16)
    gains_blocks = level_weights.reshape(PAIRED_MIXER_NUM, LEVELS, blocks, TOK_DEV).transpose(2, 0, 1, 3)
    result = lax.map(output_of, (jnp.arange(blocks, dtype=jnp.int32), values_all, in_all, out_all, local_log.transpose(1, 0, 2), gains_blocks, before.T))
    return result.reshape(STEP_AMOUNT, inner_width)
```

```python
import functools
import jax
import jax.numpy as jnp
from jax import lax
from jax.experimental import pallas as pl
from jax.experimental.pallas import tpu as pltpu
from jax.sharding import PartitionSpec as P

LANES = 128
CHUNKS = 2
MESH = pl.DeviceIdType.MESH


def bits_of(number):
    return number.bit_length()


def wide(row, times):
    return jnp.concatenate([row] * times, axis=1)


def kernel(
    seq_bits, xbc, taps, decay, lw, gain, out,
    pad, halo, in_map, out_map_t, values_t, ll, ll_col, scores_t, level_code, wt, near_t,
    agg, send, node, span, span_rx, prefix,
    halo_sem, span_send, span_recv, chip_send, chip_recv, step_send, step_recv, fwd_send, fwd_recv,
):
    rows, width = xbc.shape
    heads = decay.shape[0]
    kern = taps.shape[0]
    half = heads // 2
    piece = half // CHUNKS
    tiles = rows // LANES
    tile_bits = bits_of(LANES) - 1
    local_bits = bits_of(rows) - 1
    count = 1 << seq_bits
    me = lax.axis_index("seq")
    core = lax.rem(me, 2)
    group = lax.axis_index("groups")
    after, before = lax.rem(me + 1, count), lax.rem(me + count - 1, count)

    def bit_at(k):
        return lax.rem(lax.div(me, 1 << k), 2)

    def mate(k):
        return me + (1 - 2 * bit_at(k)) * (1 << k)

    def remote(src, dst, s, r, to):
        return pltpu.make_async_remote_copy(
            src_ref=src, dst_ref=dst, send_sem=s, recv_sem=r,
            device_id=(group, to), device_id_type=MESH,
        )

    barrier = pltpu.get_barrier_semaphore()
    for to in [after, before] + [mate(k) for k in range(seq_bits)]:
        pl.semaphore_signal(barrier, inc=1, device_id=(group, to), device_id_type=MESH)

    tri = (
        lax.broadcasted_iota(jnp.int32, (rows, rows), 0)
        <= lax.broadcasted_iota(jnp.int32, (rows, rows), 1)
    ).astype(jnp.float32).astype(jnp.bfloat16)
    rest = decay[...]
    total = jnp.zeros((heads, rows), jnp.float32)
    parts = []
    for _ in range(3):
        part = rest.astype(jnp.bfloat16)
        rest = rest - part.astype(jnp.float32)
        parts.append(part)
    for part in reversed(parts):
        total = total + jnp.dot(part, tri, preferred_element_type=jnp.float32)
    for h in range(heads):
        ll[h] = total[h : h + 1]
    span[0] = jnp.broadcast_to(total[:, rows - 1 :], (heads, LANES))
    flipped = jnp.transpose(
        jnp.concatenate([total, jnp.zeros((LANES - heads, rows), jnp.float32)], axis=0)
    )
    for h in range(heads):
        ll_col[h] = jnp.broadcast_to(flipped[:, h : h + 1], (rows, LANES))
    s_pos = lax.broadcasted_iota(jnp.int32, (LANES, LANES), 0)
    t_pos = lax.broadcasted_iota(jnp.int32, (LANES, LANES), 1)
    differ = jnp.bitwise_xor(s_pos, t_pos)
    code = jnp.zeros((LANES, LANES), jnp.int32)
    for p in range(tile_bits):
        code = code + (differ >= 1 << p).astype(jnp.int32)
    level_code[...] = code

    @pl.loop(0, width // LANES)
    def _(j):
        at = pl.ds(pl.multiple_of(j * LANES, LANES), LANES)
        pad[j, 8 : 8 + rows, :] = xbc[:, at].astype(jnp.float32)

    pl.semaphore_wait(barrier, 2 + seq_bits)

    halo_copy = remote(
        xbc.at[rows - 16 : rows, :], halo, halo_sem.at[0], halo_sem.at[1], after
    )
    halo_copy.start()

    def span_copy(k):
        return remote(span.at[k], span_rx.at[k], span_send.at[k], span_recv.at[k], mate(k))

    span_copy(0).start()
    halo_copy.wait()

    @pl.loop(0, width // LANES)
    def _(j):
        at = pl.ds(pl.multiple_of(j * LANES, LANES), LANES)
        pad[j, 0:8, :] = jnp.where(me == 0, 0.0, halo[:, at].astype(jnp.float32)[8:16])

    def conv(j):
        at = pl.ds(pl.multiple_of(j * LANES, LANES), LANES)
        weights = taps[:, at]
        first = 8 - kern + 1
        total = pad[j, first : first + rows, :] * weights[0:1]
        for k in range(1, kern):
            total = total + pad[j, first + k : first + k + rows, :] * weights[k : k + 1]
        return (total / (1.0 + jnp.exp(-total))).astype(jnp.bfloat16)

    in_map[...] = conv(heads)
    out_map_t[...] = jnp.transpose(conv(heads + 1))

    def state(first):
        @pl.loop(0, piece)
        def _(i):
            h = first + i
            flipped = jnp.transpose(conv(h))
            values_t[h] = flipped
            row = ll[h]
            tail = jnp.exp(row[:, rows - 1 :] - row)
            decayed = (flipped.astype(jnp.float32) * tail).astype(jnp.bfloat16)
            st = jnp.dot(decayed, in_map[...], preferred_element_type=jnp.float32)
            agg[h] = st
            send[0, h] = st.astype(jnp.bfloat16)

    mine, theirs = core * half, (1 - core) * half

    def chip_copy(first, slot):
        at = pl.ds(first, piece)
        return remote(
            send.at[0, at], node.at[0, at], chip_send.at[slot], chip_recv.at[slot], mate(0)
        )

    def step_copy(k, q):
        at = pl.ds(mine + q * piece, piece)
        i = k * CHUNKS + q
        return remote(send.at[k, at], node.at[k, at], step_send.at[i], step_recv.at[i], mate(k))

    def fwd_copy(k, q, first):
        at = pl.ds(first + q * piece, piece)
        i = k * CHUNKS + q
        return remote(node.at[k, at], node.at[k, at], fwd_send.at[i], fwd_recv.at[i], mate(0))

    def span_step(k):
        span_copy(k).wait()
        other = span_rx[k]
        behind = prefix[k]
        prefix[k + 1] = behind + jnp.where(bit_at(k) == 1, other, 0.0)
        span[k + 1] = span[k] + other
        if k + 1 < seq_bits:
            span_copy(k + 1).start()

    def combine(k, q):
        upper = bit_at(k) == 1

        @pl.loop(0, piece)
        def _(i):
            h = mine + q * piece + i
            own_span = span[k, pl.ds(h, 1), :]
            other_span = span_rx[k, pl.ds(h, 1), :]
            keep = jnp.exp(jnp.where(upper, own_span, other_span))
            own_factor = jnp.where(upper, 1.0, keep)
            other_factor = jnp.where(upper, keep, 1.0)
            joined = agg[h] * own_factor + node[k, h].astype(jnp.float32) * other_factor
            agg[h] = joined
            send[k + 1, h] = joined.astype(jnp.bfloat16)

    prefix[0] = jnp.zeros((heads, LANES), jnp.float32)
    spans_done = 0
    for q in range(CHUNKS):
        state(theirs + q * piece)
        chip_copy(theirs + q * piece, q).start()
        if spans_done < seq_bits:
            span_step(spans_done)
            spans_done += 1
    for q in range(CHUNKS):
        state(mine + q * piece)
        chip_copy(mine + q * piece, CHUNKS + q).start()
        chip_copy(mine + q * piece, q).wait_recv()
        if seq_bits > 1:
            combine(0, q)
            step_copy(1, q).start()
        if spans_done < seq_bits:
            span_step(spans_done)
            spans_done += 1

    scored = jnp.dot(in_map[...], out_map_t[...], preferred_element_type=jnp.float32)
    s_all = lax.broadcasted_iota(jnp.int32, (rows, rows), 0)
    t_all = lax.broadcasted_iota(jnp.int32, (rows, rows), 1)
    scores_t[...] = jnp.where(s_all <= t_all, scored, 0.0)
    wt[...] = jnp.zeros_like(wt)

    def near(h):
        for a in range(tiles):
            t_at = slice(a * LANES, (a + 1) * LANES)
            row = ll[h, :, t_at]
            for b in range(a + 1):
                s_at = slice(b * LANES, (b + 1) * LANES)
                gap = row - ll_col[h, s_at, :]
                if a == b:
                    gap = jnp.minimum(gap, 0.0)
                    code = level_code[...]
                    choices = [lw[h, l : l + 1, t_at] for l in range(tile_bits + 1)]
                    bit = 0
                    while len(choices) > 1:
                        odd = jnp.bitwise_and(code, 1 << bit) != 0
                        choices = [
                            jnp.where(odd, choices[m + 1], choices[m])
                            for m in range(0, len(choices), 2)
                        ]
                        bit += 1
                    chosen = choices[0]
                else:
                    level = tile_bits + bits_of(a ^ b)
                    chosen = lw[h, level : level + 1, t_at]
                weight = chosen * jnp.exp(gap) * scores_t[s_at, t_at]
                wt[s_at, t_at] = weight.astype(jnp.bfloat16)
        for a in range(0, tiles, 2):
            deep = min(a + 2, tiles) * LANES
            t_at = slice(a * LANES, deep)
            near_t[h, :, t_at] = jnp.dot(
                values_t[h, :, 0:deep], wt[0:deep, t_at], preferred_element_type=jnp.float32
            )

    events = [(k, q) for k in range(1, seq_bits) for q in range(CHUNKS)]
    marks = [heads * i // (len(events) + 1) for i in range(len(events) + 2)]

    def event(k, q):
        if q == 0 and spans_done <= k:
            pass
        step_copy(k, q).wait_recv()
        fwd_copy(k, q, mine).start()
        if k + 1 < seq_bits:
            combine(k, q)
            step_copy(k + 1, q).start()

    for i in range(len(events) + 1):
        while i < len(events) and spans_done < seq_bits and spans_done <= events[i][0]:
            span_step(spans_done)
            spans_done += 1

        @pl.loop(marks[i], marks[i + 1])
        def _(h):
            near(h)

        if i < len(events):
            event(*events[i])

    def far(k, h):
        upper = bit_at(k) == 1
        level = local_bits + 1 + k
        exponent = ll[h] + wide(prefix[k, pl.ds(h, 1), :], tiles)
        factor = jnp.where(upper, lw[h, level : level + 1, :] * jnp.exp(exponent), 0.0)
        product = jnp.dot(node[k, h], out_map_t[...], preferred_element_type=jnp.float32)
        return product * factor

    for q in range(CHUNKS):
        chip_copy(theirs + q * piece, CHUNKS + q).wait_recv()
    for k in range(1, seq_bits):
        for q in range(CHUNKS):
            fwd_copy(k, q, theirs).wait_recv()

    @pl.loop(0, heads)
    def _(h):
        mixed = near_t[h]
        for k in range(seq_bits):
            mixed = mixed + far(k, h)
        mean = jnp.mean(mixed * mixed, axis=0, keepdims=True)
        normed = jnp.transpose(mixed * lax.rsqrt(mean + 1e-05))
        at = pl.ds(pl.multiple_of(h * LANES, LANES), LANES)
        out[:, at] = (normed * gain[pl.ds(h, 1), :]).astype(jnp.bfloat16)

    for q in range(CHUNKS):
        chip_copy(theirs + q * piece, q).wait_send()
        chip_copy(mine + q * piece, CHUNKS + q).wait_send()
    for k in range(1, seq_bits):
        for q in range(CHUNKS):
            step_copy(k, q).wait_send()
            fwd_copy(k, q, mine).wait_send()


def on_device(xbc, conv_weight, log_decay, level_weights, gain):
    rows, width = xbc.shape
    heads = log_decay.shape[0]
    inner = gain.shape[0]
    dim = inner // heads
    seq_bits = lax.axis_size("seq").bit_length() - 1
    f32, bf16 = jnp.float32, jnp.bfloat16
    dma = pltpu.SemaphoreType.DMA
    vmem = pl.BlockSpec(memory_space=pltpu.VMEM)
    square = (heads, dim, LANES)
    return pl.pallas_call(
        functools.partial(kernel, seq_bits),
        out_shape=jax.ShapeDtypeStruct((rows, inner), bf16),
        in_specs=[vmem] * 5,
        out_specs=vmem,
        scratch_shapes=[
            pltpu.VMEM((width // LANES, rows + 8, LANES), f32),
            pltpu.VMEM((16, width), bf16),
            pltpu.VMEM((rows, LANES), bf16),
            pltpu.VMEM((LANES, rows), bf16),
            pltpu.VMEM((heads, dim, rows), bf16),
            pltpu.VMEM((heads, 1, rows), f32),
            pltpu.VMEM((heads, rows, LANES), f32),
            pltpu.VMEM((rows, rows), f32),
            pltpu.VMEM((LANES, LANES), jnp.int32),
            pltpu.VMEM((rows, rows), bf16),
            pltpu.VMEM((heads, dim, rows), f32),
            pltpu.VMEM(square, f32),
            pltpu.VMEM((seq_bits,) + square, bf16),
            pltpu.VMEM((seq_bits,) + square, bf16),
            pltpu.VMEM((seq_bits + 1, heads, LANES), f32),
            pltpu.VMEM((seq_bits, heads, LANES), f32),
            pltpu.VMEM((seq_bits + 1, heads, LANES), f32),
            dma((2,)),
            dma((seq_bits,)),
            dma((seq_bits,)),
            dma((2 * CHUNKS,)),
            dma((2 * CHUNKS,)),
            dma((seq_bits * CHUNKS,)),
            dma((seq_bits * CHUNKS,)),
            dma((seq_bits * CHUNKS,)),
            dma((seq_bits * CHUNKS,)),
        ],
        compiler_params=pltpu.CompilerParams(
            collective_id=0, has_side_effects=True, vmem_limit_bytes=60 * 1024 * 1024
        ),
        name="mixer",
    )(xbc, conv_weight, log_decay, level_weights, gain.reshape(heads, dim))


def solution(mesh):
    in_specs = (
        P(("groups", "seq"), None),
        P(),
        P(None, ("groups", "seq")),
        P(None, None, ("groups", "seq")),
        P(),
    )
    out_specs = P(("groups", "seq"), None)
    return jax.shard_map(
        on_device, mesh=mesh, in_specs=in_specs, out_specs=out_specs, check_vma=False
    )
```

```python
import functools
import jax
import jax.numpy as jnp
from jax import lax
from jax.experimental import pallas as pl
from jax.experimental.pallas import tpu as pltpu
from jax.sharding import PartitionSpec as P

LANES = 128
CHUNKS = 4
MESH = pl.DeviceIdType.MESH


def bits_of(number):
    return number.bit_length()


def wide(row, times):
    return jnp.concatenate([row] * times, axis=1)


def kernel(
    seq_bits, xbc, taps, decay, lw_in, gain, out,
    lw, pad, halo, in_map, out_map_t, values_t, ll, ll_col, scores_t, level_code, wt, near_t,
    agg, send, node, span, span_rx, prefix,
    halo_sem, span_send, span_recv, chip_send, chip_recv, step_send, step_recv, fwd_send, fwd_recv,
):
    rows, width = xbc.shape
    heads = decay.shape[0]
    kern = taps.shape[0]
    half = heads // 2
    piece = half // CHUNKS
    tiles = rows // LANES
    tile_bits = bits_of(LANES) - 1
    local_bits = bits_of(rows) - 1
    count = 1 << seq_bits
    me = lax.axis_index("seq")
    core = lax.rem(me, 2)
    group = lax.axis_index("groups")
    after, before = lax.rem(me + 1, count), lax.rem(me + count - 1, count)
    reach = count // 4
    quarter = lax.div(me, reach)
    last = seq_bits - 1
    ahead, behind = lax.rem(me + reach, count), lax.rem(me + count - reach, count)

    def bit_at(k):
        return lax.rem(lax.div(me, 1 << k), 2)

    def mate(k):
        return me + (1 - 2 * bit_at(k)) * (1 << k)

    def remote(src, dst, s, r, to):
        return pltpu.make_async_remote_copy(
            src_ref=src, dst_ref=dst, send_sem=s, recv_sem=r,
            device_id=(group, to), device_id_type=MESH,
        )

    barrier = pltpu.get_barrier_semaphore()
    for to in [after, before, ahead, behind] + [mate(k) for k in range(seq_bits)]:
        pl.semaphore_signal(barrier, inc=1, device_id=(group, to), device_id_type=MESH)

    @pl.loop(0, width // LANES)
    def _(j):
        at = pl.ds(pl.multiple_of(j * LANES, LANES), LANES)
        pad[j, 8 : 8 + rows, :] = xbc[:, at].astype(jnp.float32)

    pl.semaphore_wait(barrier, 4 + seq_bits)

    halo_copy = remote(
        xbc.at[rows - 8 : rows, :], halo, halo_sem.at[0], halo_sem.at[1], after
    )

    @pl.when(me < count - 1)
    def _():
        halo_copy.start()

    for h in range(heads):
        for l in range(lw_in.shape[0]):
            lw[h, l : l + 1, :] = lw_in[l, h : h + 1, :]
    wt[...] = jnp.zeros_like(wt)

    tri = (
        lax.broadcasted_iota(jnp.int32, (rows, rows), 0)
        <= lax.broadcasted_iota(jnp.int32, (rows, rows), 1)
    ).astype(jnp.float32).astype(jnp.bfloat16)
    rest = decay[...]
    total = jnp.zeros((heads, rows), jnp.float32)
    parts = []
    for _ in range(3):
        part = rest.astype(jnp.bfloat16)
        rest = rest - part.astype(jnp.float32)
        parts.append(part)
    for part in reversed(parts):
        total = total + jnp.dot(part, tri, preferred_element_type=jnp.float32)
    for h in range(heads):
        ll[h] = total[h : h + 1]
    span[0] = jnp.broadcast_to(total[:, rows - 1 :], (heads, LANES))
    def span_copy(k):
        return remote(span.at[k], span_rx.at[k], span_send.at[k], span_recv.at[k], mate(k))

    span_copy(0).start()
    flipped = jnp.transpose(
        jnp.concatenate([total, jnp.zeros((LANES - heads, rows), jnp.float32)], axis=0)
    )
    for h in range(heads):
        ll_col[h] = jnp.broadcast_to(flipped[:, h : h + 1], (rows, LANES))
    s_pos = lax.broadcasted_iota(jnp.int32, (LANES, LANES), 0)
    t_pos = lax.broadcasted_iota(jnp.int32, (LANES, LANES), 1)
    differ = jnp.bitwise_xor(s_pos, t_pos)
    code = jnp.zeros((LANES, LANES), jnp.int32)
    for p in range(tile_bits):
        code = code + (differ >= 1 << p).astype(jnp.int32)
    level_code[...] = code


    @pl.when(me > 0)
    def _():
        halo_copy.wait_recv()


    @pl.loop(0, width // LANES)
    def _(j):
        at = pl.ds(pl.multiple_of(j * LANES, LANES), LANES)
        pad[j, 0:8, :] = jnp.where(me == 0, 0.0, halo[:, at].astype(jnp.float32))

    def conv(j):
        at = pl.ds(pl.multiple_of(j * LANES, LANES), LANES)
        weights = taps[:, at]
        first = 8 - kern + 1
        total = pad[j, first : first + rows, :] * weights[0:1]
        for k in range(1, kern):
            total = total + pad[j, first + k : first + k + rows, :] * weights[k : k + 1]
        return (total / (1.0 + jnp.exp(-total))).astype(jnp.bfloat16)

    in_map[...] = conv(heads)
    out_map_t[...] = jnp.transpose(conv(heads + 1))

    def state(first):
        @pl.loop(0, piece)
        def _(i):
            h = first + i
            flipped = jnp.transpose(conv(h))
            values_t[h] = flipped
            row = ll[h]
            tail = jnp.exp(row[:, rows - 1 :] - row)
            decayed = (flipped.astype(jnp.float32) * tail).astype(jnp.bfloat16)
            st = jnp.dot(decayed, in_map[...], preferred_element_type=jnp.float32)
            agg[h] = st
            send[0, h] = st.astype(jnp.bfloat16)

    mine, theirs = core * half, (1 - core) * half

    def chip_copy(first, slot):
        at = pl.ds(first, piece)
        return remote(
            send.at[0, at], node.at[0, at], chip_send.at[slot], chip_recv.at[slot], mate(0)
        )

    def step_copy(k, q):
        at = pl.ds(mine + q * piece, piece)
        i = k * CHUNKS + q
        return remote(send.at[k, at], node.at[k, at], step_send.at[i], step_recv.at[i], mate(k))

    def last_copy(q, source):
        at = pl.ds(mine + q * piece, piece)
        i = last * CHUNKS + q
        return remote(
            source.at[last, at], node.at[last, at], step_send.at[i], step_recv.at[i], ahead
        )

    def fwd_copy(k, q, first):
        at = pl.ds(first + q * piece, piece)
        i = k * CHUNKS + q
        return remote(node.at[k, at], node.at[k, at], fwd_send.at[i], fwd_recv.at[i], mate(0))

    def span_step(k):
        span_copy(k).wait_recv()
        other = span_rx[k]
        prefix[k + 1] = prefix[k] + jnp.where(bit_at(k) == 1, other, 0.0)
        span[k + 1] = span[k] + other
        if k + 1 < seq_bits:
            span_copy(k + 1).start()

    def combine(k, q):
        upper = bit_at(k) == 1

        @pl.loop(0, piece)
        def _(i):
            h = mine + q * piece + i
            own_span = span[k, pl.ds(h, 1), :]
            other_span = span_rx[k, pl.ds(h, 1), :]
            keep = jnp.exp(jnp.where(upper, own_span, other_span))
            own_factor = jnp.where(upper, 1.0, keep)
            other_factor = jnp.where(upper, keep, 1.0)
            joined = agg[h] * own_factor + node[k, h].astype(jnp.float32) * other_factor
            agg[h] = joined
            send[k + 1, h] = joined.astype(jnp.bfloat16)

    prefix[0] = jnp.zeros((heads, LANES), jnp.float32)

    def ship(k, q):
        if k < last:
            step_copy(k, q).start()
        else:
            @pl.when(quarter == 1)
            def _():
                last_copy(q, send).start()

    def join(k, q):
        if q == 0:
            span_step(k)
        if k + 1 < last:
            combine(k, q)
        elif k + 1 == last:
            @pl.when(quarter == 1)
            def _():
                combine(k, q)
        if k + 1 <= last:
            ship(k + 1, q)

    for q in range(CHUNKS):
        state(theirs + q * piece)
        chip_copy(theirs + q * piece, q).start()
        if q > 0:
            chip_copy(mine + (q - 1) * piece, q - 1).wait_recv()
            join(0, q - 1)
        state(mine + q * piece)
        chip_copy(mine + q * piece, CHUNKS + q).start()
    chip_copy(mine + (CHUNKS - 1) * piece, CHUNKS - 1).wait_recv()
    join(0, CHUNKS - 1)

    scored = jnp.dot(in_map[...], out_map_t[...], preferred_element_type=jnp.float32)
    s_all = lax.broadcasted_iota(jnp.int32, (rows, rows), 0)
    t_all = lax.broadcasted_iota(jnp.int32, (rows, rows), 1)
    scores_t[...] = jnp.where(s_all <= t_all, scored, 0.0)

    def near(h):
        for a in range(tiles):
            t_at = slice(a * LANES, (a + 1) * LANES)
            row = ll[h, :, t_at]
            for b in range(a + 1):
                s_at = slice(b * LANES, (b + 1) * LANES)
                gap = row - ll_col[h, s_at, :]
                if a == b:
                    gap = jnp.minimum(gap, 0.0)
                    code = level_code[...]
                    choices = [lw[h, l : l + 1, t_at] for l in range(tile_bits + 1)]
                    bit = 0
                    while len(choices) > 1:
                        odd = jnp.bitwise_and(code, 1 << bit) != 0
                        choices = [
                            jnp.where(odd, choices[m + 1], choices[m])
                            for m in range(0, len(choices), 2)
                        ]
                        bit += 1
                    chosen = choices[0]
                else:
                    level = tile_bits + bits_of(a ^ b)
                    chosen = lw[h, level : level + 1, t_at]
                weight = chosen * jnp.exp(gap) * scores_t[s_at, t_at]
                wt[s_at, t_at] = weight.astype(jnp.bfloat16)
        for a in range(0, tiles, 2):
            deep = min(a + 2, tiles) * LANES
            t_at = slice(a * LANES, deep)
            near_t[h, :, t_at] = jnp.dot(
                values_t[h, :, 0:deep], wt[0:deep, t_at], preferred_element_type=jnp.float32
            )

    events = sorted(
        ((k, q) for k in range(1, last) for q in range(CHUNKS)), key=lambda e: (2 * e[0] + e[1], e)
    )
    marks = [heads * i // len(events) for i in range(len(events) + 1)]
    for i, (k, q) in enumerate(events):
        @pl.loop(marks[i], marks[i + 1])
        def _(h):
            near(h)

        step_copy(k, q).wait_recv()
        join(k, q)
        fwd_copy(k, q, mine).start()

    def far(k, h):
        upper = bit_at(k) == 1
        level = local_bits + 1 + k
        exponent = ll[h] + wide(prefix[k, pl.ds(h, 1), :], tiles)
        factor = jnp.where(upper, lw[h, level : level + 1, :] * jnp.exp(exponent), 0.0)
        source = node[k, h]
        if k == last:
            source = jnp.where(upper, source, jnp.zeros_like(source))
        product = jnp.dot(source, out_map_t[...], preferred_element_type=jnp.float32)
        return product * factor

    def finish(first):
        @pl.loop(0, piece)
        def _(i):
            h = first + i
            mixed = near_t[h]
            for k in range(seq_bits):
                mixed = mixed + far(k, h)
            mean = jnp.mean(mixed * mixed, axis=0, keepdims=True)
            normed = jnp.transpose(mixed * lax.rsqrt(mean + 1e-05))
            at = pl.ds(pl.multiple_of(h * LANES, LANES), LANES)
            out[:, at] = (normed * gain[pl.ds(h, 1), :]).astype(jnp.bfloat16)

    def finish_theirs(q):
        chip_copy(theirs + q * piece, CHUNKS + q).wait_recv()
        for k in range(1, last):
            fwd_copy(k, q, theirs).wait_recv()

        @pl.when(quarter >= 2)
        def _():
            fwd_copy(last, q, theirs).wait_recv()

        finish(theirs + q * piece)

    span_step(last)
    for q in range(CHUNKS):
        @pl.when(quarter >= 2)
        def _():
            last_copy(q, send).wait_recv()

        @pl.when(quarter == 2)
        def _():
            last_copy(q, node).start()

        @pl.when(quarter >= 2)
        def _():
            fwd_copy(last, q, mine).start()

        if q > 1:
            finish_theirs(q - 2)
        finish(mine + q * piece)
    for q in range(max(CHUNKS - 2, 0), CHUNKS):
        finish_theirs(q)

    @pl.when(me < count - 1)
    def _():
        halo_copy.wait_send()

    for k in range(seq_bits):
        span_copy(k).wait_send()
    for q in range(CHUNKS):
        chip_copy(theirs + q * piece, q).wait_send()
        chip_copy(mine + q * piece, CHUNKS + q).wait_send()
        for k in range(1, last):
            step_copy(k, q).wait_send()
            fwd_copy(k, q, mine).wait_send()

        @pl.when(quarter == 1)
        def _():
            last_copy(q, send).wait_send()

        @pl.when(quarter == 2)
        def _():
            last_copy(q, node).wait_send()

        @pl.when(quarter >= 2)
        def _():
            fwd_copy(last, q, mine).wait_send()


def on_device(xbc, conv_weight, log_decay, level_weights, gain):
    rows, width = xbc.shape
    heads = log_decay.shape[0]
    inner = gain.shape[0]
    dim = inner // heads
    seq_bits = lax.axis_size("seq").bit_length() - 1
    f32, bf16 = jnp.float32, jnp.bfloat16
    dma = pltpu.SemaphoreType.DMA
    vmem = pl.BlockSpec(memory_space=pltpu.VMEM)
    square = (heads, dim, LANES)
    return pl.pallas_call(
        functools.partial(kernel, seq_bits),
        out_shape=jax.ShapeDtypeStruct((rows, inner), bf16),
        in_specs=[vmem] * 5,
        out_specs=vmem,
        scratch_shapes=[
            pltpu.VMEM((heads, level_weights.shape[1], rows), f32),
            pltpu.VMEM((width // LANES, rows + 8, LANES), f32),
            pltpu.VMEM((8, width), bf16),
            pltpu.VMEM((rows, LANES), bf16),
            pltpu.VMEM((LANES, rows), bf16),
            pltpu.VMEM((heads, dim, rows), bf16),
            pltpu.VMEM((heads, 1, rows), f32),
            pltpu.VMEM((heads, rows, LANES), f32),
            pltpu.VMEM((rows, rows), f32),
            pltpu.VMEM((LANES, LANES), jnp.int32),
            pltpu.VMEM((rows, rows), bf16),
            pltpu.VMEM((heads, dim, rows), f32),
            pltpu.VMEM(square, f32),
            pltpu.VMEM((seq_bits,) + square, bf16),
            pltpu.VMEM((seq_bits,) + square, bf16),
            pltpu.VMEM((seq_bits + 1, heads, LANES), f32),
            pltpu.VMEM((seq_bits, heads, LANES), f32),
            pltpu.VMEM((seq_bits + 1, heads, LANES), f32),
            dma((2,)),
            dma((seq_bits,)),
            dma((seq_bits,)),
            dma((2 * CHUNKS,)),
            dma((2 * CHUNKS,)),
            dma((seq_bits * CHUNKS,)),
            dma((seq_bits * CHUNKS,)),
            dma((seq_bits * CHUNKS,)),
            dma((seq_bits * CHUNKS,)),
        ],
        compiler_params=pltpu.CompilerParams(
            collective_id=0, has_side_effects=True, vmem_limit_bytes=36 * 1024 * 1024
        ),
        name="mixer",
    )(xbc, conv_weight, log_decay, level_weights.transpose(1, 0, 2), gain.reshape(heads, dim))


def solution(mesh):
    in_specs = (
        P(("groups", "seq"), None),
        P(),
        P(None, ("groups", "seq")),
        P(None, None, ("groups", "seq")),
        P(),
    )
    out_specs = P(("groups", "seq"), None)
    return jax.shard_map(
        on_device, mesh=mesh, in_specs=in_specs, out_specs=out_specs, check_vma=False
    )
```

```python
import functools
import jax
import jax.numpy as jnp
from jax import lax
from jax.experimental import pallas as pl
from jax.experimental.pallas import tpu as pltpu
from jax.sharding import PartitionSpec as P

LANES = 128
CHUNKS = 8
MESH = pl.DeviceIdType.MESH


def bits_of(number):
    return number.bit_length()


def wide(row, times):
    return jnp.concatenate([row] * times, axis=1)


def kernel(
    seq_bits, xbc_hbm, taps_hbm, decay_hbm, lw_hbm, gain_hbm, out,
    xbc, taps, decay, lw_in, gain, load_sem, lw, pad, halo, in_map, out_map_t, values_t, ll, ll_col, scores_t, level_code, wt, near_t,
    agg, send, node, span, span_rx, prefix,
    halo_sem, span_send, span_recv, chip_send, chip_recv, step_send, step_recv, fwd_send, fwd_recv,
):
    rows, width = xbc.shape
    heads = decay.shape[0]
    kern = taps.shape[0]
    half = heads // 2
    piece = half // CHUNKS
    tiles = rows // LANES
    tile_bits = bits_of(LANES) - 1
    local_bits = bits_of(rows) - 1
    count = 1 << seq_bits
    me = lax.axis_index("seq")
    core = lax.rem(me, 2)
    group = lax.axis_index("groups")
    after, before = lax.rem(me + 1, count), lax.rem(me + count - 1, count)
    reach = count // 4
    quarter = lax.div(me, reach)
    last = seq_bits - 1
    ahead, behind = lax.rem(me + reach, count), lax.rem(me + count - reach, count)

    def bit_at(k):
        return lax.rem(lax.div(me, 1 << k), 2)

    def mate(k):
        return me + (1 - 2 * bit_at(k)) * (1 << k)

    def remote(src, dst, s, r, to):
        return pltpu.make_async_remote_copy(
            src_ref=src, dst_ref=dst, send_sem=s, recv_sem=r,
            device_id=(group, to), device_id_type=MESH,
        )

    loads = [
        pltpu.make_async_copy(src, dst, load_sem.at[i])
        for i, (src, dst) in enumerate((
            (decay_hbm, decay), (xbc_hbm, xbc), (lw_hbm, lw_in), (taps_hbm, taps), (gain_hbm, gain)
        ))
    ]
    for load in loads:
        load.start()
    barrier = pltpu.get_barrier_semaphore()
    for to in [after, before, ahead, behind] + [mate(k) for k in range(seq_bits)]:
        pl.semaphore_signal(barrier, inc=1, device_id=(group, to), device_id_type=MESH)

    tri = (
        lax.broadcasted_iota(jnp.int32, (rows, rows), 0)
        <= lax.broadcasted_iota(jnp.int32, (rows, rows), 1)
    ).astype(jnp.float32).astype(jnp.bfloat16)
    loads[0].wait()
    rest = decay[...]
    total = jnp.zeros((heads, rows), jnp.float32)
    parts = []
    for _ in range(3):
        part = rest.astype(jnp.bfloat16)
        rest = rest - part.astype(jnp.float32)
        parts.append(part)
    for part in reversed(parts):
        total = total + jnp.dot(part, tri, preferred_element_type=jnp.float32)
    for h in range(heads):
        ll[h] = total[h : h + 1]
    span[0] = jnp.broadcast_to(total[:, rows - 1 :], (heads, LANES))
    pl.semaphore_wait(barrier, 4 + seq_bits)

    halo_copy = remote(
        xbc_hbm.at[rows - 8 : rows, :], halo, halo_sem.at[0], halo_sem.at[1], after
    )

    @pl.when(me < count - 1)
    def _():
        halo_copy.start()

    def span_copy(k):
        return remote(span.at[k], span_rx.at[k], span_send.at[k], span_recv.at[k], mate(k))

    span_copy(0).start()
    loads[1].wait()

    @pl.loop(0, width // LANES)
    def _(j):
        at = pl.ds(pl.multiple_of(j * LANES, LANES), LANES)
        pad[j, 8 : 8 + rows, :] = xbc[:, at].astype(jnp.float32)

    loads[2].wait()
    for h in range(heads):
        for l in range(lw_in.shape[0]):
            lw[h, l : l + 1, :] = lw_in[l, h : h + 1, :]
    wt[...] = jnp.zeros_like(wt)
    loads[3].wait()
    loads[4].wait()
    flipped = jnp.transpose(
        jnp.concatenate([total, jnp.zeros((LANES - heads, rows), jnp.float32)], axis=0)
    )
    for h in range(heads):
        ll_col[h] = jnp.broadcast_to(flipped[:, h : h + 1], (rows, LANES))
    s_pos = lax.broadcasted_iota(jnp.int32, (LANES, LANES), 0)
    t_pos = lax.broadcasted_iota(jnp.int32, (LANES, LANES), 1)
    differ = jnp.bitwise_xor(s_pos, t_pos)
    code = jnp.zeros((LANES, LANES), jnp.int32)
    for p in range(tile_bits):
        code = code + (differ >= 1 << p).astype(jnp.int32)
    level_code[...] = code


    @pl.when(me > 0)
    def _():
        halo_copy.wait_recv()


    @pl.loop(0, width // LANES)
    def _(j):
        at = pl.ds(pl.multiple_of(j * LANES, LANES), LANES)
        pad[j, 0:8, :] = jnp.where(me == 0, 0.0, halo[:, at].astype(jnp.float32))

    def conv(j):
        at = pl.ds(pl.multiple_of(j * LANES, LANES), LANES)
        weights = taps[:, at]
        first = 8 - kern + 1
        total = pad[j, first : first + rows, :] * weights[0:1]
        for k in range(1, kern):
            total = total + pad[j, first + k : first + k + rows, :] * weights[k : k + 1]
        return (total / (1.0 + jnp.exp(-total))).astype(jnp.bfloat16)

    in_map[...] = conv(heads)
    out_map_t[...] = jnp.transpose(conv(heads + 1))

    def state(first):
        @pl.loop(0, piece)
        def _(i):
            h = first + i
            flipped = jnp.transpose(conv(h))
            values_t[h] = flipped
            row = ll[h]
            tail = jnp.exp(row[:, rows - 1 :] - row)
            decayed = (flipped.astype(jnp.float32) * tail).astype(jnp.bfloat16)
            st = jnp.dot(decayed, in_map[...], preferred_element_type=jnp.float32)
            agg[h] = st
            send[0, h] = st.astype(jnp.bfloat16)

    mine, theirs = core * half, (1 - core) * half

    def chip_copy(first, slot):
        at = pl.ds(first, piece)
        return remote(
            send.at[0, at], node.at[0, at], chip_send.at[slot], chip_recv.at[slot], mate(0)
        )

    def step_copy(k, q):
        at = pl.ds(mine + q * piece, piece)
        i = k * CHUNKS + q
        return remote(send.at[k, at], node.at[k, at], step_send.at[i], step_recv.at[i], mate(k))

    def last_copy(q, source):
        at = pl.ds(mine + q * piece, piece)
        i = last * CHUNKS + q
        return remote(
            source.at[last, at], node.at[last, at], step_send.at[i], step_recv.at[i], ahead
        )

    def fwd_copy(k, q, first):
        at = pl.ds(first + q * piece, piece)
        i = k * CHUNKS + q
        return remote(node.at[k, at], node.at[k, at], fwd_send.at[i], fwd_recv.at[i], mate(0))

    def span_step(k):
        span_copy(k).wait_recv()
        other = span_rx[k]
        prefix[k + 1] = prefix[k] + jnp.where(bit_at(k) == 1, other, 0.0)
        span[k + 1] = span[k] + other
        if k + 1 < seq_bits:
            span_copy(k + 1).start()

    def combine(k, q):
        upper = bit_at(k) == 1

        @pl.loop(0, piece)
        def _(i):
            h = mine + q * piece + i
            own_span = span[k, pl.ds(h, 1), :]
            other_span = span_rx[k, pl.ds(h, 1), :]
            keep = jnp.exp(jnp.where(upper, own_span, other_span))
            own_factor = jnp.where(upper, 1.0, keep)
            other_factor = jnp.where(upper, keep, 1.0)
            joined = agg[h] * own_factor + node[k, h].astype(jnp.float32) * other_factor
            agg[h] = joined
            send[k + 1, h] = joined.astype(jnp.bfloat16)

    prefix[0] = jnp.zeros((heads, LANES), jnp.float32)

    def ship(k, q):
        if k < last:
            step_copy(k, q).start()
        else:
            @pl.when(quarter == 1)
            def _():
                last_copy(q, send).start()

    def join(k, q):
        if q == 0:
            span_step(k)
        if k + 1 < last:
            combine(k, q)
        elif k + 1 == last:
            @pl.when(quarter == 1)
            def _():
                combine(k, q)
        if k + 1 <= last:
            ship(k + 1, q)

    for q in range(CHUNKS):
        state(theirs + q * piece)
        chip_copy(theirs + q * piece, q).start()
        if q > 0:
            chip_copy(mine + (q - 1) * piece, q - 1).wait_recv()
            join(0, q - 1)
        state(mine + q * piece)
        chip_copy(mine + q * piece, CHUNKS + q).start()
    chip_copy(mine + (CHUNKS - 1) * piece, CHUNKS - 1).wait_recv()
    join(0, CHUNKS - 1)

    scored = jnp.dot(in_map[...], out_map_t[...], preferred_element_type=jnp.float32)
    s_all = lax.broadcasted_iota(jnp.int32, (rows, rows), 0)
    t_all = lax.broadcasted_iota(jnp.int32, (rows, rows), 1)
    scores_t[...] = jnp.where(s_all <= t_all, scored, 0.0)

    def near(h):
        for a in range(tiles):
            t_at = slice(a * LANES, (a + 1) * LANES)
            row = ll[h, :, t_at]
            for b in range(a + 1):
                s_at = slice(b * LANES, (b + 1) * LANES)
                gap = row - ll_col[h, s_at, :]
                if a == b:
                    gap = jnp.minimum(gap, 0.0)
                    code = level_code[...]
                    choices = [lw[h, l : l + 1, t_at] for l in range(tile_bits + 1)]
                    bit = 0
                    while len(choices) > 1:
                        odd = jnp.bitwise_and(code, 1 << bit) != 0
                        choices = [
                            jnp.where(odd, choices[m + 1], choices[m])
                            for m in range(0, len(choices), 2)
                        ]
                        bit += 1
                    chosen = choices[0]
                else:
                    level = tile_bits + bits_of(a ^ b)
                    chosen = lw[h, level : level + 1, t_at]
                weight = chosen * jnp.exp(gap) * scores_t[s_at, t_at]
                wt[s_at, t_at] = weight.astype(jnp.bfloat16)
        for a in range(0, tiles, 2):
            deep = min(a + 2, tiles) * LANES
            t_at = slice(a * LANES, deep)
            near_t[h, :, t_at] = jnp.dot(
                values_t[h, :, 0:deep], wt[0:deep, t_at], preferred_element_type=jnp.float32
            )

    events = sorted(
        ((k, q) for k in range(1, last) for q in range(CHUNKS)), key=lambda e: (3 * e[0] + e[1], e)
    )
    marks = [heads * i // len(events) for i in range(len(events) + 1)]
    for i, (k, q) in enumerate(events):
        @pl.loop(marks[i], marks[i + 1])
        def _(h):
            near(h)

        step_copy(k, q).wait_recv()
        join(k, q)
        fwd_copy(k, q, mine).start()

    def far(k, h):
        upper = bit_at(k) == 1
        level = local_bits + 1 + k
        exponent = ll[h] + wide(prefix[k, pl.ds(h, 1), :], tiles)
        factor = jnp.where(upper, lw[h, level : level + 1, :] * jnp.exp(exponent), 0.0)
        source = node[k, h]
        if k == last:
            source = jnp.where(upper, source, jnp.zeros_like(source))
        product = jnp.dot(source, out_map_t[...], preferred_element_type=jnp.float32)
        return product * factor

    def finish(first):
        @pl.loop(0, piece)
        def _(i):
            h = first + i
            mixed = near_t[h]
            for k in range(seq_bits):
                mixed = mixed + far(k, h)
            mean = jnp.mean(mixed * mixed, axis=0, keepdims=True)
            normed = jnp.transpose(mixed * lax.rsqrt(mean + 1e-05))
            at = pl.ds(pl.multiple_of(h * LANES, LANES), LANES)
            out[:, at] = (normed * gain[pl.ds(h, 1), :]).astype(jnp.bfloat16)

    def finish_theirs(q):
        chip_copy(theirs + q * piece, CHUNKS + q).wait_recv()
        for k in range(1, last):
            fwd_copy(k, q, theirs).wait_recv()

        @pl.when(quarter >= 2)
        def _():
            fwd_copy(last, q, theirs).wait_recv()

        finish(theirs + q * piece)

    span_step(last)
    for q in range(CHUNKS):
        @pl.when(quarter >= 2)
        def _():
            last_copy(q, send).wait_recv()

        @pl.when(quarter == 2)
        def _():
            last_copy(q, node).start()

        @pl.when(quarter >= 2)
        def _():
            fwd_copy(last, q, mine).start()

        if q > 1:
            finish_theirs(q - 2)
        finish(mine + q * piece)
    for q in range(max(CHUNKS - 2, 0), CHUNKS):
        finish_theirs(q)

    @pl.when(me < count - 1)
    def _():
        halo_copy.wait_send()

    for k in range(seq_bits):
        span_copy(k).wait_send()
    for q in range(CHUNKS):
        chip_copy(theirs + q * piece, q).wait_send()
        chip_copy(mine + q * piece, CHUNKS + q).wait_send()
        for k in range(1, last):
            step_copy(k, q).wait_send()
            fwd_copy(k, q, mine).wait_send()

        @pl.when(quarter == 1)
        def _():
            last_copy(q, send).wait_send()

        @pl.when(quarter == 2)
        def _():
            last_copy(q, node).wait_send()

        @pl.when(quarter >= 2)
        def _():
            fwd_copy(last, q, mine).wait_send()


def on_device(xbc, conv_weight, log_decay, level_weights, gain):
    rows, width = xbc.shape
    heads = log_decay.shape[0]
    inner = gain.shape[0]
    dim = inner // heads
    seq_bits = lax.axis_size("seq").bit_length() - 1
    f32, bf16 = jnp.float32, jnp.bfloat16
    dma = pltpu.SemaphoreType.DMA
    vmem = pl.BlockSpec(memory_space=pltpu.VMEM)
    hbm = pl.BlockSpec(memory_space=pltpu.HBM)
    square = (heads, dim, LANES)
    return pl.pallas_call(
        functools.partial(kernel, seq_bits),
        out_shape=jax.ShapeDtypeStruct((rows, inner), bf16),
        in_specs=[hbm] * 5,
        out_specs=vmem,
        scratch_shapes=[
            pltpu.VMEM((rows, width), bf16),
            pltpu.VMEM(conv_weight.shape, f32),
            pltpu.VMEM((heads, rows), f32),
            pltpu.VMEM((level_weights.shape[1], heads, rows), f32),
            pltpu.VMEM((heads, dim), f32),
            dma((5,)),
            pltpu.VMEM((heads, level_weights.shape[1], rows), f32),
            pltpu.VMEM((width // LANES, rows + 8, LANES), f32),
            pltpu.VMEM((8, width), bf16),
            pltpu.VMEM((rows, LANES), bf16),
            pltpu.VMEM((LANES, rows), bf16),
            pltpu.VMEM((heads, dim, rows), bf16),
            pltpu.VMEM((heads, 1, rows), f32),
            pltpu.VMEM((heads, rows, LANES), f32),
            pltpu.VMEM((rows, rows), f32),
            pltpu.VMEM((LANES, LANES), jnp.int32),
            pltpu.VMEM((rows, rows), bf16),
            pltpu.VMEM((heads, dim, rows), f32),
            pltpu.VMEM(square, f32),
            pltpu.VMEM((seq_bits,) + square, bf16),
            pltpu.VMEM((seq_bits,) + square, bf16),
            pltpu.VMEM((seq_bits + 1, heads, LANES), f32),
            pltpu.VMEM((seq_bits, heads, LANES), f32),
            pltpu.VMEM((seq_bits + 1, heads, LANES), f32),
            dma((2,)),
            dma((seq_bits,)),
            dma((seq_bits,)),
            dma((2 * CHUNKS,)),
            dma((2 * CHUNKS,)),
            dma((seq_bits * CHUNKS,)),
            dma((seq_bits * CHUNKS,)),
            dma((seq_bits * CHUNKS,)),
            dma((seq_bits * CHUNKS,)),
        ],
        compiler_params=pltpu.CompilerParams(
            collective_id=0, has_side_effects=True, vmem_limit_bytes=60 * 1024 * 1024
        ),
        name="mixer",
    )(xbc, conv_weight, log_decay, level_weights.transpose(1, 0, 2), gain.reshape(heads, dim))


def solution(mesh):
    in_specs = (
        P(("groups", "seq"), None),
        P(),
        P(None, ("groups", "seq")),
        P(None, None, ("groups", "seq")),
        P(),
    )
    out_specs = P(("groups", "seq"), None)
    return jax.shard_map(
        on_device, mesh=mesh, in_specs=in_specs, out_specs=out_specs, check_vma=False
    )
```

```python
import functools
import jax
import jax.numpy as jnp
from jax import lax
from jax.experimental import pallas as pl
from jax.experimental.pallas import tpu as pltpu
from jax.sharding import PartitionSpec as P

LANES = 128
CHUNKS = 8
MESH = pl.DeviceIdType.MESH


def bits_of(number):
    return number.bit_length()


def wide(row, times):
    return jnp.concatenate([row] * times, axis=1)


def kernel(
    seq_bits, xbc_hbm, taps_hbm, decay_hbm, lw_hbm, gain_hbm, out_hbm,
    out, out_sem, xbc, taps, decay, lw_in, gain, load_sem, lw, pad, halo, in_map, out_map_t, values_t, ll, ll_col, scores_t, level_code, wt, near_t,
    agg, send, node, span, span_rx, prefix,
    halo_sem, span_send, span_recv, chip_send, chip_recv, step_send, step_recv, fwd_send, fwd_recv,
):
    rows, width = xbc.shape
    heads = decay.shape[0]
    kern = taps.shape[0]
    half = heads // 2
    piece = half // CHUNKS
    tiles = rows // LANES
    tile_bits = bits_of(LANES) - 1
    local_bits = bits_of(rows) - 1
    count = 1 << seq_bits
    me = lax.axis_index("seq")
    core = lax.rem(me, 2)
    group = lax.axis_index("groups")
    after, before = lax.rem(me + 1, count), lax.rem(me + count - 1, count)
    reach = count // 4
    quarter = lax.div(me, reach)
    last = seq_bits - 1
    ahead, behind = lax.rem(me + reach, count), lax.rem(me + count - reach, count)

    def bit_at(k):
        return lax.rem(lax.div(me, 1 << k), 2)

    def mate(k):
        return me + (1 - 2 * bit_at(k)) * (1 << k)

    def remote(src, dst, s, r, to):
        return pltpu.make_async_remote_copy(
            src_ref=src, dst_ref=dst, send_sem=s, recv_sem=r,
            device_id=(group, to), device_id_type=MESH,
        )

    loads = [
        pltpu.make_async_copy(src, dst, load_sem.at[i])
        for i, (src, dst) in enumerate((
            (decay_hbm, decay), (xbc_hbm, xbc), (lw_hbm, lw_in), (taps_hbm, taps), (gain_hbm, gain)
        ))
    ]
    for load in loads:
        load.start()
    barrier = pltpu.get_barrier_semaphore()
    for to in [after, before, ahead, behind] + [mate(k) for k in range(seq_bits)]:
        pl.semaphore_signal(barrier, inc=1, device_id=(group, to), device_id_type=MESH)

    tri = (
        lax.broadcasted_iota(jnp.int32, (rows, rows), 0)
        <= lax.broadcasted_iota(jnp.int32, (rows, rows), 1)
    ).astype(jnp.float32).astype(jnp.bfloat16)
    loads[0].wait()
    rest = decay[...]
    total = jnp.zeros((heads, rows), jnp.float32)
    parts = []
    for _ in range(3):
        part = rest.astype(jnp.bfloat16)
        rest = rest - part.astype(jnp.float32)
        parts.append(part)
    for part in reversed(parts):
        total = total + jnp.dot(part, tri, preferred_element_type=jnp.float32)
    for h in range(heads):
        ll[h] = total[h : h + 1]
    span[0] = jnp.broadcast_to(total[:, rows - 1 :], (heads, LANES))
    pl.semaphore_wait(barrier, 4 + seq_bits)

    halo_copy = remote(
        xbc_hbm.at[rows - 8 : rows, :], halo, halo_sem.at[0], halo_sem.at[1], after
    )

    @pl.when(me < count - 1)
    def _():
        halo_copy.start()

    def span_copy(k):
        return remote(span.at[k], span_rx.at[k], span_send.at[k], span_recv.at[k], mate(k))

    span_copy(0).start()
    loads[1].wait()

    @pl.loop(0, width // LANES)
    def _(j):
        at = pl.ds(pl.multiple_of(j * LANES, LANES), LANES)
        pad[j, 8 : 8 + rows, :] = xbc[:, at].astype(jnp.float32)

    loads[2].wait()
    for h in range(heads):
        for l in range(lw_in.shape[0]):
            lw[h, l : l + 1, :] = lw_in[l, h : h + 1, :]
    wt[...] = jnp.zeros_like(wt)
    loads[3].wait()
    loads[4].wait()
    flipped = jnp.transpose(
        jnp.concatenate([total, jnp.zeros((LANES - heads, rows), jnp.float32)], axis=0)
    )
    for h in range(heads):
        ll_col[h] = jnp.broadcast_to(flipped[:, h : h + 1], (rows, LANES))
    s_pos = lax.broadcasted_iota(jnp.int32, (LANES, LANES), 0)
    t_pos = lax.broadcasted_iota(jnp.int32, (LANES, LANES), 1)
    differ = jnp.bitwise_xor(s_pos, t_pos)
    code = jnp.zeros((LANES, LANES), jnp.int32)
    for p in range(tile_bits):
        code = code + (differ >= 1 << p).astype(jnp.int32)
    level_code[...] = code


    @pl.when(me > 0)
    def _():
        halo_copy.wait_recv()


    @pl.loop(0, width // LANES)
    def _(j):
        at = pl.ds(pl.multiple_of(j * LANES, LANES), LANES)
        pad[j, 0:8, :] = jnp.where(me == 0, 0.0, halo[:, at].astype(jnp.float32))

    def conv(j):
        at = pl.ds(pl.multiple_of(j * LANES, LANES), LANES)
        weights = taps[:, at]
        first = 8 - kern + 1
        total = pad[j, first : first + rows, :] * weights[0:1]
        for k in range(1, kern):
            total = total + pad[j, first + k : first + k + rows, :] * weights[k : k + 1]
        return (total / (1.0 + jnp.exp(-total))).astype(jnp.bfloat16)

    in_map[...] = conv(heads)
    out_map_t[...] = jnp.transpose(conv(heads + 1))

    def state(first):
        @pl.loop(0, piece)
        def _(i):
            h = first + i
            flipped = jnp.transpose(conv(h))
            values_t[h] = flipped
            row = ll[h]
            tail = jnp.exp(row[:, rows - 1 :] - row)
            decayed = (flipped.astype(jnp.float32) * tail).astype(jnp.bfloat16)
            st = jnp.dot(decayed, in_map[...], preferred_element_type=jnp.float32)
            agg[h] = st
            send[0, h] = st.astype(jnp.bfloat16)

    mine, theirs = core * half, (1 - core) * half

    def chip_copy(first, slot):
        at = pl.ds(first, piece)
        return remote(
            send.at[0, at], node.at[0, at], chip_send.at[slot], chip_recv.at[slot], mate(0)
        )

    def step_copy(k, q):
        at = pl.ds(mine + q * piece, piece)
        i = k * CHUNKS + q
        return remote(send.at[k, at], node.at[k, at], step_send.at[i], step_recv.at[i], mate(k))

    def last_copy(q, source):
        at = pl.ds(mine + q * piece, piece)
        i = last * CHUNKS + q
        return remote(
            source.at[last, at], node.at[last, at], step_send.at[i], step_recv.at[i], ahead
        )

    def fwd_copy(k, q, first):
        at = pl.ds(first + q * piece, piece)
        i = k * CHUNKS + q
        return remote(node.at[k, at], node.at[k, at], fwd_send.at[i], fwd_recv.at[i], mate(0))

    def span_step(k):
        span_copy(k).wait_recv()
        other = span_rx[k]
        prefix[k + 1] = prefix[k] + jnp.where(bit_at(k) == 1, other, 0.0)
        span[k + 1] = span[k] + other
        if k + 1 < seq_bits:
            span_copy(k + 1).start()

    def combine(k, q):
        upper = bit_at(k) == 1

        @pl.loop(0, piece)
        def _(i):
            h = mine + q * piece + i
            own_span = span[k, pl.ds(h, 1), :]
            other_span = span_rx[k, pl.ds(h, 1), :]
            keep = jnp.exp(jnp.where(upper, own_span, other_span))
            own_factor = jnp.where(upper, 1.0, keep)
            other_factor = jnp.where(upper, keep, 1.0)
            joined = agg[h] * own_factor + node[k, h].astype(jnp.float32) * other_factor
            agg[h] = joined
            send[k + 1, h] = joined.astype(jnp.bfloat16)

    prefix[0] = jnp.zeros((heads, LANES), jnp.float32)

    def ship(k, q):
        if k < last:
            step_copy(k, q).start()
        else:
            @pl.when(quarter == 1)
            def _():
                last_copy(q, send).start()

    def join(k, q):
        if q == 0:
            span_step(k)
        if k + 1 < last:
            combine(k, q)
        elif k + 1 == last:
            @pl.when(quarter == 1)
            def _():
                combine(k, q)
        if k + 1 <= last:
            ship(k + 1, q)

    for q in range(CHUNKS):
        state(theirs + q * piece)
        chip_copy(theirs + q * piece, q).start()
        if q > 0:
            chip_copy(mine + (q - 1) * piece, q - 1).wait_recv()
            join(0, q - 1)
        state(mine + q * piece)
        chip_copy(mine + q * piece, CHUNKS + q).start()
    chip_copy(mine + (CHUNKS - 1) * piece, CHUNKS - 1).wait_recv()
    join(0, CHUNKS - 1)

    scored = jnp.dot(in_map[...], out_map_t[...], preferred_element_type=jnp.float32)
    s_all = lax.broadcasted_iota(jnp.int32, (rows, rows), 0)
    t_all = lax.broadcasted_iota(jnp.int32, (rows, rows), 1)
    scores_t[...] = jnp.where(s_all <= t_all, scored, 0.0)

    def near(h):
        for a in range(tiles):
            t_at = slice(a * LANES, (a + 1) * LANES)
            row = ll[h, :, t_at]
            for b in range(a + 1):
                s_at = slice(b * LANES, (b + 1) * LANES)
                gap = row - ll_col[h, s_at, :]
                if a == b:
                    gap = jnp.minimum(gap, 0.0)
                    code = level_code[...]
                    choices = [lw[h, l : l + 1, t_at] for l in range(tile_bits + 1)]
                    bit = 0
                    while len(choices) > 1:
                        odd = jnp.bitwise_and(code, 1 << bit) != 0
                        choices = [
                            jnp.where(odd, choices[m + 1], choices[m])
                            for m in range(0, len(choices), 2)
                        ]
                        bit += 1
                    chosen = choices[0]
                else:
                    level = tile_bits + bits_of(a ^ b)
                    chosen = lw[h, level : level + 1, t_at]
                weight = chosen * jnp.exp(gap) * scores_t[s_at, t_at]
                wt[s_at, t_at] = weight.astype(jnp.bfloat16)
        for a in range(0, tiles, 2):
            deep = min(a + 2, tiles) * LANES
            t_at = slice(a * LANES, deep)
            near_t[h, :, t_at] = jnp.dot(
                values_t[h, :, 0:deep], wt[0:deep, t_at], preferred_element_type=jnp.float32
            )

    events = sorted(
        ((k, q) for k in range(1, last) for q in range(CHUNKS)), key=lambda e: (3 * e[0] + e[1], e)
    )
    marks = [heads * i // len(events) for i in range(len(events) + 1)]
    for i, (k, q) in enumerate(events):
        @pl.loop(marks[i], marks[i + 1])
        def _(h):
            near(h)

        step_copy(k, q).wait_recv()
        join(k, q)
        fwd_copy(k, q, mine).start()

    def far(k, h):
        upper = bit_at(k) == 1
        level = local_bits + 1 + k
        exponent = ll[h] + wide(prefix[k, pl.ds(h, 1), :], tiles)
        factor = jnp.where(upper, lw[h, level : level + 1, :] * jnp.exp(exponent), 0.0)
        source = node[k, h]
        if k == last:
            source = jnp.where(upper, source, jnp.zeros_like(source))
        product = jnp.dot(source, out_map_t[...], preferred_element_type=jnp.float32)
        return product * factor

    def out_copy(h):
        at = pl.ds(pl.multiple_of(h * LANES, LANES), LANES)
        return pltpu.make_async_copy(out.at[:, at], out_hbm.at[:, at], out_sem.at[h])

    def finish(first):
        @pl.loop(0, piece)
        def _(i):
            h = first + i
            mixed = near_t[h]
            for k in range(seq_bits):
                mixed = mixed + far(k, h)
            mean = jnp.mean(mixed * mixed, axis=0, keepdims=True)
            normed = jnp.transpose(mixed * lax.rsqrt(mean + 1e-05))
            at = pl.ds(pl.multiple_of(h * LANES, LANES), LANES)
            out[:, at] = (normed * gain[pl.ds(h, 1), :]).astype(jnp.bfloat16)
            out_copy(h).start()

    def finish_theirs(q):
        chip_copy(theirs + q * piece, CHUNKS + q).wait_recv()
        for k in range(1, last):
            fwd_copy(k, q, theirs).wait_recv()

        @pl.when(quarter >= 2)
        def _():
            fwd_copy(last, q, theirs).wait_recv()

        finish(theirs + q * piece)

    span_step(last)
    for q in range(CHUNKS):
        @pl.when(quarter >= 2)
        def _():
            last_copy(q, send).wait_recv()

        @pl.when(quarter == 2)
        def _():
            last_copy(q, node).start()

        @pl.when(quarter >= 2)
        def _():
            fwd_copy(last, q, mine).start()

        if q > 1:
            finish_theirs(q - 2)
        finish(mine + q * piece)
    for q in range(max(CHUNKS - 2, 0), CHUNKS):
        finish_theirs(q)

    @pl.loop(0, heads)
    def _(h):
        out_copy(h).wait()

    @pl.when(me < count - 1)
    def _():
        halo_copy.wait_send()

    for k in range(seq_bits):
        span_copy(k).wait_send()
    for q in range(CHUNKS):
        chip_copy(theirs + q * piece, q).wait_send()
        chip_copy(mine + q * piece, CHUNKS + q).wait_send()
        for k in range(1, last):
            step_copy(k, q).wait_send()
            fwd_copy(k, q, mine).wait_send()

        @pl.when(quarter == 1)
        def _():
            last_copy(q, send).wait_send()

        @pl.when(quarter == 2)
        def _():
            last_copy(q, node).wait_send()

        @pl.when(quarter >= 2)
        def _():
            fwd_copy(last, q, mine).wait_send()


def on_device(xbc, conv_weight, log_decay, level_weights, gain):
    rows, width = xbc.shape
    heads = log_decay.shape[0]
    inner = gain.shape[0]
    dim = inner // heads
    seq_bits = lax.axis_size("seq").bit_length() - 1
    f32, bf16 = jnp.float32, jnp.bfloat16
    dma = pltpu.SemaphoreType.DMA
    hbm = pl.BlockSpec(memory_space=pltpu.HBM)
    square = (heads, dim, LANES)
    return pl.pallas_call(
        functools.partial(kernel, seq_bits),
        out_shape=jax.ShapeDtypeStruct((rows, inner), bf16),
        in_specs=[hbm] * 5,
        out_specs=hbm,
        scratch_shapes=[
            pltpu.VMEM((rows, inner), bf16),
            dma((heads,)),
            pltpu.VMEM((rows, width), bf16),
            pltpu.VMEM(conv_weight.shape, f32),
            pltpu.VMEM((heads, rows), f32),
            pltpu.VMEM((level_weights.shape[1], heads, rows), f32),
            pltpu.VMEM((heads, dim), f32),
            dma((5,)),
            pltpu.VMEM((heads, level_weights.shape[1], rows), f32),
            pltpu.VMEM((width // LANES, rows + 8, LANES), f32),
            pltpu.VMEM((8, width), bf16),
            pltpu.VMEM((rows, LANES), bf16),
            pltpu.VMEM((LANES, rows), bf16),
            pltpu.VMEM((heads, dim, rows), bf16),
            pltpu.VMEM((heads, 1, rows), f32),
            pltpu.VMEM((heads, rows, LANES), f32),
            pltpu.VMEM((rows, rows), f32),
            pltpu.VMEM((LANES, LANES), jnp.int32),
            pltpu.VMEM((rows, rows), bf16),
            pltpu.VMEM((heads, dim, rows), f32),
            pltpu.VMEM(square, f32),
            pltpu.VMEM((seq_bits,) + square, bf16),
            pltpu.VMEM((seq_bits,) + square, bf16),
            pltpu.VMEM((seq_bits + 1, heads, LANES), f32),
            pltpu.VMEM((seq_bits, heads, LANES), f32),
            pltpu.VMEM((seq_bits + 1, heads, LANES), f32),
            dma((2,)),
            dma((seq_bits,)),
            dma((seq_bits,)),
            dma((2 * CHUNKS,)),
            dma((2 * CHUNKS,)),
            dma((seq_bits * CHUNKS,)),
            dma((seq_bits * CHUNKS,)),
            dma((seq_bits * CHUNKS,)),
            dma((seq_bits * CHUNKS,)),
        ],
        compiler_params=pltpu.CompilerParams(
            collective_id=0, has_side_effects=True, vmem_limit_bytes=60 * 1024 * 1024
        ),
        name="mixer",
    )(xbc, conv_weight, log_decay, level_weights.transpose(1, 0, 2), gain.reshape(heads, dim))


def solution(mesh):
    in_specs = (
        P(("groups", "seq"), None),
        P(),
        P(None, ("groups", "seq")),
        P(None, None, ("groups", "seq")),
        P(),
    )
    out_specs = P(("groups", "seq"), None)
    return jax.shard_map(
        on_device, mesh=mesh, in_specs=in_specs, out_specs=out_specs, check_vma=False
    )
```
